128 devices in a mesh: row: 8 (over z, core), col: 16 (over y, x).
Axes of the slice: x: 4, y: 4, z: 4, core: 2. Of those that a mesh axis runs over, the one named last changes fastest.
Arguments:
- panel_blocks: bfloat16 [16, 8, 512, 512], P('col', None, 'row'), may hold values from -0.25 to 0.25
- factor_inverse: bfloat16 [16, 512, 512], P('col')
- target_rows: int32 [16, 8], replicated, may hold values from 0 to 15, as said below
- owner_order: int32 [16], replicated, may hold values from 0 to 15, each once
- ancestor_rows: float32 [16, 512, 8192], P('col', 'row'), may hold values from -1.8 to 1.8
Outputs:
- updated_rows: float32 [16, 512, 8192], P('col', 'row')
The draws below stay inside these ranges and needn't reach their ends.
Inputs may be any that keep to these rules, and one draw needn't show every extreme that they name: `target_rows`: each row names 8 different ancestor block rows in ascending order; each index of col holds exactly one supernode. `owner_order`: each ancestor block row once.
All inputs are finite; a program needn't handle non-finite values.
Results may differ from the reference program's by a relative error of at most 0.0024.
Values may be sent and summed in bfloat16 or wider, within the bound.
A program may use at most 192 MiB of HBM per device.

```python
import math
import jax
import jax.numpy as jnp
from jax import lax

W = 512
PB = 8
SN_DEV = 1
NSUP = 16
NA = 16


def draw_factor_inverse(key, part):
    first_key, second_key = jax.random.split(key)
    shape_full = (NSUP, W, W)
    lower = jax.random.normal(first_key, shape_full, jnp.float32)
    diagonal = jax.random.uniform(second_key, (NSUP, W, 1), jnp.float32, 0.5, 1.5)
    lower = lower * (1.0 / math.sqrt(W))
    row_index = lax.broadcasted_iota(jnp.int32, shape_full, 1)
    col_index = lax.broadcasted_iota(jnp.int32, shape_full, 2)
    result = jnp.where(row_index > col_index, lower, jnp.where(row_index == col_index, diagonal, 0.0))
    return result.astype(jnp.bfloat16)


def draw_target_rows(key, part):
    groups = NSUP // SN_DEV
    group_keys = jax.random.split(key, groups)
    orders = jax.vmap(lambda k: jax.random.permutation(k, NA))(group_keys)
    member = lax.broadcasted_iota(jnp.int32, (SN_DEV, PB), 0)
    within = lax.broadcasted_iota(jnp.int32, (SN_DEV, PB), 1)
    places = (member * PB + within) % NA
    picked = orders[:, places]
    picked = jnp.sort(picked, axis=2)
    return picked.reshape(NSUP, PB).astype(jnp.int32)


def shard_levels(own_key, extent, cuts, least, high):
    level, own = 1.0, jax.random.fold_in(own_key, 6)
    for position, blocks in cuts:
        steps = jnp.exp(jax.random.uniform(jax.random.fold_in(own, position), (blocks,), jnp.float32, least / len(cuts), high / len(cuts)))
        level = level * jnp.repeat(steps, extent[position] // blocks).reshape([-1 if axis == position else 1 for axis in range(len(extent))])
    return level


def bell_draw(key, extent, deviation, reach, cuts=(), held_as=jnp.bfloat16):
    array = deviation * jax.random.normal(key, extent, jnp.float32)
    if cuts:
        array = array * shard_levels(key, extent, cuts, -0.22, 0.18)
    return jnp.clip(array, -reach, reach).astype(held_as)


def setup_inputs(seed: int = 0) -> dict:
    streams_of = jax.random.split(jax.random.key(seed), 6)
    panel_blocks = bell_draw(streams_of[0], (NSUP, PB, W, W), W ** -0.5, 0.25, ((0, 16), (2, 8)))
    factor_inverse = draw_factor_inverse(jax.random.fold_in(streams_of[5], 71), 0)
    target_rows = draw_target_rows(jax.random.fold_in(streams_of[5], 71), 0)
    owner_order = jax.random.permutation(streams_of[3], NA).astype(jnp.int32)
    ancestor_rows = bell_draw(streams_of[4], (NA, W, NA * W), 0.3, 1.8, ((0, 16), (1, 8)), jnp.float32)
    return {"panel_blocks": panel_blocks, "factor_inverse": factor_inverse, "target_rows": target_rows, "owner_order": owner_order, "ancestor_rows": ancestor_rows}


def reference(panel_blocks, factor_inverse, target_rows, owner_order, ancestor_rows):
    def one_supernode(carry, inputs):
        blocks, inverse, targets = inputs
        solved = jnp.einsum('piw,vw->piv', blocks.astype(jnp.float32), inverse.astype(jnp.float32)).astype(jnp.bfloat16)
        solved_wide = solved.astype(jnp.float32)
        product = jnp.einsum('piw,qmw->piqm', solved_wide, solved_wide).astype(jnp.bfloat16)
        product = lax.optimization_barrier(product).astype(jnp.float32)
        carry = carry.at[targets[:, None], :, targets[None, :], :].add(jnp.transpose(product, (0, 2, 1, 3)))
        return carry, None

    zeros_init = jnp.zeros((NA, W, NA, W), jnp.float32)
    update, _ = lax.scan(one_supernode, zeros_init, (panel_blocks, factor_inverse, target_rows))
    ordered = update[owner_order].reshape(NA, W, NA * W)
    return ancestor_rows - ordered
```

```python
import jax
import jax.numpy as jnp
from jax import lax
from jax.sharding import PartitionSpec as P


def body(panel_blocks, factor_inverse, target_rows, owner_order, ancestor_rows):
    col_size = lax.axis_size("col")
    width = panel_blocks.shape[3]
    ancestors = owner_order.shape[0]
    col_place = lax.axis_index("col")
    own_targets = lax.dynamic_slice_in_dim(target_rows, col_place, 1, 0)[0]
    own_solved = jnp.einsum(
        "piw,vw->piv", panel_blocks[0], factor_inverse[0], preferred_element_type=jnp.float32
    ).astype(jnp.bfloat16)
    full_solved = lax.all_gather(own_solved, "row", axis=1, tiled=True)
    products = jnp.einsum(
        "piw,qmw->piqm", own_solved, full_solved, preferred_element_type=jnp.float32
    ).astype(jnp.bfloat16)
    matched = own_targets[None, :] == owner_order[:, None]
    places = lax.broadcasted_iota(jnp.int32, matched.shape, 1)
    position = jnp.sum(jnp.where(matched, places, 0), axis=1)
    present = jnp.any(matched, axis=1)
    send = jnp.where(present[:, None, None, None], products[position], jnp.zeros((), products.dtype))
    received = lax.all_to_all(send, "col", 0, 0, tiled=True)
    block_ids = lax.broadcasted_iota(jnp.int32, (1, 1, ancestors), 2)
    onehot = (target_rows[:, :, None] == block_ids).astype(jnp.bfloat16)
    update = jnp.einsum("sqb,siqm->ibm", onehot, received, preferred_element_type=jnp.float32)
    return ancestor_rows - update.reshape(ancestor_rows.shape)


def solution(mesh):
    return jax.shard_map(
        body,
        mesh=mesh,
        in_specs=(
            P("col", None, "row", None),
            P("col", None, None),
            P(),
            P(),
            P("col", "row", None),
        ),
        out_specs=P("col", "row", None),
        check_vma=False,
    )
```
